32 devices in a mesh: parts: 2 (over y), db: 4 (over z), blk: 4 (over x, core).
Axes of the slice: x: 2, y: 2, z: 4, core: 2. Of those that a mesh axis runs over, the one named last changes fastest.
Arguments:
- queries: bfloat16 [8192, 768], P(('parts', 'db', 'blk')), parts along dimension 0, may hold values from -6 to 6
- projection: bfloat16 [768, 768], replicated, may hold values from -0.21875 to 0.21875
- vectors: bfloat16 [768, 32768], P(None, ('parts', 'db', 'blk')), parts along dimension 1, may hold values from -0.21875 to 0.21875
- bins: int32 [32768], P(('parts', 'db', 'blk')), parts along dimension 0, may hold values from 0 to 127, as said below
- routes: int32 [8192, 1], P(('parts', 'db', 'blk')), parts along dimension 0, may hold values from 0 to 3; in each aligned block of 256 rows (0 to 255, 256 to 511, ...) at most 128 rows name the same one
Outputs:
- best: float32 [8192, 128], P(('parts', 'db', 'blk')), parts along dimension 0
The draws below stay inside these ranges and needn't reach their ends.
There are 2 independent parts, one for each index of `parts`. The reference program is written for one: setup_inputs(seed, part) draws one part's arguments, and reference() takes and returns one part's arrays. A program takes and returns all parts, laid end to end along the dimension named above; an argument that names none is the same for every part. Nothing has to cross between parts.
Inputs may be any that keep to these rules, and one draw needn't show every extreme that they name: Within every aligned block of 1024 entries each of the 128 bins occurs exactly 1024 // 128 times. `routes`: within every aligned block of 256 rows no group is named by more than 128 rows; in every draw some block names some group exactly 128 times.
All inputs are finite; a program needn't handle non-finite values.
Results may differ from the reference program's by a relative error of at most 0.0014.
Values may be sent and summed in bfloat16 or wider, within the bound.
A program may use at most 64 MiB of HBM per device.

```python
import math
import jax
import jax.numpy as jnp
import numpy as np
from jax import lax

D = 768
BINS = 128
REQ_DEV = 256
VEC_DEV = 1024
CAP = 128
REQUESTS = 4096
VECTORS = 16384
N_DB = 4
N_BLK = 4


def draw_bins(key, part):
    blocks_total = VECTORS // VEC_DEV
    block_keys = jax.random.split(jax.random.fold_in(key, 7), blocks_total)
    pattern = jnp.arange(VEC_DEV, dtype=jnp.int32) % BINS

    def shuffle_block(block_key):
        return jax.random.permutation(block_key, pattern)
    return jax.vmap(shuffle_block)(block_keys).reshape(-1)


def level_of(key, dims, shards, smallest, high):
    def one(dim, shards_of):
        steps = jax.random.uniform(jax.random.fold_in(jax.random.fold_in(key, 6), dim), (shards_of,), jnp.float32, smallest / len(shards), high / len(shards))
        return jnp.repeat(jnp.exp(steps), dims[dim] // shards_of).reshape((-1,) + (1,) * (len(dims) - dim - 1))

    level = one(*shards[0])
    for cut in shards[1:]:
        level = level * one(*cut)
    return level


def assign_block(stream_key, own, number, rows, count, top, limit, slope):
    order = jax.random.permutation(stream_key, count)
    packed, usual = portions_of(count, rows * top, limit, slope, True), portions_of(count, rows * top, limit, slope, False)
    places = jnp.arange(count)

    def named(sizes, offset_by):
        used = int((sizes > 0).sum())
        fixed = max(1, used // 4)
        shifted = fixed + (places - fixed + offset_by * (used - fixed)) % max(1, count - fixed)
        return jnp.zeros((count,), jnp.int32).at[order[jnp.where(places < fixed, places, shifted)]].set(jnp.asarray(sizes, jnp.int32))

    sizes = jnp.where(number % 4 == 0, named(packed, number // 4), named(usual, number - number // 4 - 1))
    mixed = jax.random.permutation(jax.random.fold_in(own, 3), count)
    source_of, receiver = mixed[0:count // 2 * 2:2], mixed[1:count // 2 * 2:2]
    margin = jnp.minimum(sizes[source_of] - 1, limit - sizes[receiver]) // 2
    margin = jnp.where((source_of == order[0]) | (receiver == order[0]) | (sizes[receiver] == 0), 0, jnp.maximum(margin, 0))
    shifted = jax.random.randint(jax.random.fold_in(own, 4), (count // 2,), 0, 1 << 20) % (margin + 1)
    sizes = sizes.at[source_of].add(-shifted).at[receiver].add(shifted)
    items = jnp.searchsorted(jnp.cumsum(sizes), jnp.arange(rows * top), side="right").astype(jnp.int32)
    table = items.reshape(top, rows).T
    table = table[jax.random.permutation(jax.random.fold_in(own, 1), rows)]
    offset_by = jax.random.randint(jax.random.fold_in(own, 2), (rows, 1), 0, top)
    return jnp.take_along_axis(table, (jnp.arange(top)[None, :] + offset_by) % top, axis=1)


def portions_of(count, total, bound, skew, full):
    portions = [(1 << 20) // math.isqrt(grade ** skew) + 1 for grade in range(1, count + 1)]
    largest = bound if full else min(bound, max(-(-total // count), total * portions[0] // sum(portions)))
    least = 1 if total - largest >= count - 1 else 0
    holding, rest = [largest] + [least] * (count - 1), total - largest - least * (count - 1)
    while rest > 0:
        movable = [i for i in range(1, count) if holding[i] < largest] or [i for i in range(1, count) if holding[i] < bound]
        mass, left = sum([portions[i] for i in movable]), rest
        for i in movable:
            addition = min(bound - holding[i], max(1, left * portions[i] // mass), rest)
            holding[i] = holding[i] + addition
            rest = rest - addition
    return np.array(holding)


def scatter_about(own_key, shape, scale, limit, shards=(), kind=jnp.bfloat16):
    drawn = scale * jax.random.normal(own_key, shape, jnp.float32)
    if shards:
        drawn = drawn * level_of(own_key, shape, shards, -0.22, 0.18)
    return jnp.clip(drawn, -limit, limit).astype(kind)


def setup_inputs(seed: int = 0, part: int = 0) -> dict:
    streams_of = jax.random.split(jax.random.key(seed), 6)
    part_keys = jax.random.split(jax.random.fold_in(streams_of[5], part), 6)
    queries = scatter_about(part_keys[0], (REQUESTS, D), 1.0, 6.0, ((0, 16),))
    projection = scatter_about(streams_of[1], (D, D), D ** -0.5, 0.21875)
    vectors = scatter_about(part_keys[2], (D, VECTORS), (D ** -0.5), 0.21875, ((1, 16),))
    bins = draw_bins(jax.random.fold_in(jax.random.fold_in(streams_of[5], part), 71), part)
    routes_keys = jax.random.split(jax.random.fold_in(part_keys[4], 1), REQUESTS // REQ_DEV)
    routes_turns = jax.random.permutation(jax.random.fold_in(part_keys[4], 3), REQUESTS // REQ_DEV)
    routes = jax.vmap(lambda own, number: assign_block(jax.random.fold_in(part_keys[4], 2), own, number, REQ_DEV, N_DB, 1, CAP, 2))(routes_keys, routes_turns).reshape((REQUESTS, 1))
    return {"queries": queries, "projection": projection, "vectors": vectors, "bins": bins, "routes": routes}


logit_scale = 10.0

def reference(queries, projection, vectors, bins, routes):
    devices_all = N_DB * N_BLK
    capacity = 2 * REQ_DEV // N_DB
    per_bin = VEC_DEV // BINS
    projected = jnp.dot(queries, projection, preferred_element_type=jnp.float32)
    normed = (projected * lax.rsqrt(lax.optimization_barrier(jnp.sum(projected * projected, axis=1, keepdims=True)) + 1e-06)).astype(jnp.bfloat16)
    target = routes[:, 0].reshape(devices_all, REQ_DEV)
    one_hot = (target[:, :, None] == jnp.arange(N_DB, dtype=jnp.int32)[None, None, :]).astype(jnp.int32)
    slot_index = lax.optimization_barrier(jnp.sum((jnp.cumsum(one_hot, axis=1) - one_hot) * one_hot, axis=2))
    requester = jnp.arange(devices_all, dtype=jnp.int32)[:, None]
    position = (target * (devices_all * capacity) + requester * capacity + slot_index).reshape(-1).astype(jnp.int32)
    dispatched = jnp.zeros((N_DB * devices_all * capacity, D), jnp.float32).at[position].set(normed.astype(jnp.float32))
    dispatched = dispatched.reshape(N_DB, devices_all * capacity, D)
    slab_all = vectors.reshape(D, devices_all, VEC_DEV)
    ordering = jnp.argsort(bins.reshape(devices_all, VEC_DEV), axis=1, stable=True).astype(jnp.int32)
    ordering = ordering.reshape(devices_all, BINS, per_bin).transpose(0, 2, 1).reshape(devices_all, VEC_DEV)
    sorted_all = jnp.take_along_axis(slab_all, ordering[None, :, :], axis=2)
    sorted_all = sorted_all.reshape(D, N_DB, N_BLK * VEC_DEV).transpose(1, 0, 2)

    def group_max(operands):
        query_rows, group_slab = operands
        scores = jnp.dot(query_rows, group_slab.astype(jnp.float32), preferred_element_type=jnp.float32)
        return logit_scale * lax.optimization_barrier(jnp.max(scores.reshape(query_rows.shape[0], N_BLK * per_bin, BINS), axis=1))
    maxima = lax.map(group_max, (dispatched, sorted_all))
    return maxima.reshape(-1, BINS)[position]
```

```python
import functools

import jax
import jax.numpy as jnp
from jax import lax
from jax.experimental import pallas as pl
from jax.experimental.pallas import tpu as pltpu
from jax.sharding import PartitionSpec as P

BINS = 128
TILE = 256
logit_scale = 10.0
MESH = pl.DeviceIdType.MESH


def kernel(
    G, NB, C, R,
    q_hbm, p_hbm, v_hbm, bins_ref, routes_ref,
    out_ref,
    q_ref, p_ref, raw, slab, chooser, outgoing, rows, own, xout, xin, back, ans,
    load_sem, z_ss, z_rs, x_ss, x_rs, s_ss, s_rs, xb_ss, xb_rs, zb_ss, zb_rs,
):
    H = NB // 2
    n, depth = q_ref.shape
    width = raw.shape[1]
    tiles = width // TILE
    f32, bf16 = jnp.float32, jnp.bfloat16
    d = lax.axis_index("db")
    k = lax.axis_index("blk")

    loads = [
        pltpu.make_async_copy(q_hbm, q_ref, load_sem.at[0]),
        pltpu.make_async_copy(p_hbm, p_ref, load_sem.at[1]),
        pltpu.make_async_copy(v_hbm, raw, load_sem.at[2]),
    ]
    for load in loads:
        load.start()

    barrier = pltpu.get_barrier_semaphore()
    for o in range(1, G):
        pl.semaphore_signal(barrier, inc=1, device_id={"db": d ^ o}, device_id_type=MESH)
    for h in range(1, H):
        pl.semaphore_signal(barrier, inc=1, device_id={"blk": k ^ (2 * h)}, device_id_type=MESH)
    pl.semaphore_signal(barrier, inc=1, device_id={"blk": k ^ 1}, device_id_type=MESH)

    def block(c, h, o):
        return rows.at[c, pl.ds((h * G + o) * R, R)]

    def z_copy(c, o):
        return pltpu.make_async_remote_copy(
            src_ref=outgoing.at[c, pl.ds(o * R, R)], dst_ref=block(c, 0, o),
            send_sem=z_ss.at[c, o], recv_sem=z_rs.at[c, o],
            device_id={"db": d ^ o}, device_id_type=MESH)

    def x_copy(c, h, o, step):
        return pltpu.make_async_remote_copy(
            src_ref=block(c, h, o), dst_ref=block(c, h + step, o),
            send_sem=x_ss.at[c, h + step, o], recv_sem=x_rs.at[c, h + step, o],
            device_id={"blk": k ^ (2 * step)}, device_id_type=MESH)

    def s_copy(t):
        return pltpu.make_async_remote_copy(
            src_ref=slab.at[0, t], dst_ref=slab.at[1, t],
            send_sem=s_ss.at[t], recv_sem=s_rs.at[t],
            device_id={"blk": k ^ 1}, device_id_type=MESH)

    def xb_copy(c, h):
        return pltpu.make_async_remote_copy(
            src_ref=xout.at[c, h - 1], dst_ref=xin.at[c, h - 1],
            send_sem=xb_ss.at[c, h], recv_sem=xb_rs.at[c, h],
            device_id={"blk": k ^ (2 * h)}, device_id_type=MESH)

    def zb_copy(c, o):
        return pltpu.make_async_remote_copy(
            src_ref=back.at[c, pl.ds(o * R, R)], dst_ref=ans.at[c, pl.ds(o * R, R)],
            send_sem=zb_ss.at[c, o], recv_sem=zb_rs.at[c, o],
            device_id={"db": d ^ o}, device_id_type=MESH)

    started = []

    def start(copy):
        copy.start()
        started.append(copy)

    target = routes_ref[...]
    pad = max(8, G)
    hot = jnp.where(lax.broadcasted_iota(jnp.int32, (pad, n), 0) == target, 1.0, 0.0)
    before = jnp.where(
        lax.broadcasted_iota(jnp.int32, (n, n), 0) < lax.broadcasted_iota(jnp.int32, (n, n), 1),
        1.0, 0.0).astype(bf16)
    earlier = jnp.dot(hot.astype(bf16), before, preferred_element_type=f32)
    slot = jnp.sum(hot * earlier, axis=0, keepdims=True).astype(jnp.int32)
    position = (slot // R) * (G * R) + (target ^ d) * R + slot % R

    loads[0].wait()
    loads[1].wait()
    projected = jnp.dot(q_ref[...], p_ref[...], preferred_element_type=f32)
    normed = (
        projected * lax.rsqrt(jnp.sum(projected * projected, axis=1, keepdims=True) + 1e-06)
    ).astype(bf16)

    pl.semaphore_wait(barrier, G - 1 + H)

    for c in range(C):
        pick = jnp.where(
            lax.broadcasted_iota(jnp.int32, (G * R, n), 0) + c * G * R == position, 1.0, 0.0
        ).astype(bf16)
        chooser[pl.ds(c * G * R, G * R), :] = pick
        chosen = jnp.dot(pick, normed, preferred_element_type=f32).astype(bf16)
        outgoing[c] = chosen
        rows[c, pl.ds(0, R)] = chosen[:R]
        for o in range(G - 1, 0, -1):
            start(z_copy(c, o))
        if H > 1:
            start(x_copy(c, 0, 0, 1))

    loads[2].wait()
    bins = bins_ref[...]
    inner = jnp.where(
        lax.broadcasted_iota(jnp.int32, (BINS, BINS), 0)
        < lax.broadcasted_iota(jnp.int32, (BINS, BINS), 1), 1.0, 0.0).astype(bf16)
    run = jnp.zeros((BINS, 1), f32)
    places = []
    for s in range(width // BINS):
        mine = bins[:, s * BINS:(s + 1) * BINS]
        hot = jnp.where(lax.broadcasted_iota(jnp.int32, (BINS, BINS), 0) == mine, 1.0, 0.0)
        earlier = jnp.dot(hot.astype(bf16), inner, preferred_element_type=f32) + run
        rank = jnp.sum(hot * earlier, axis=0, keepdims=True).astype(jnp.int32)
        places.append(rank * BINS + mine)
        run = run + jnp.sum(hot, axis=1, keepdims=True)
    place = jnp.concatenate(places, axis=1)
    for t in range(tiles):
        move = jnp.where(
            lax.broadcasted_iota(jnp.int32, (TILE, width), 0) + t * TILE == place, 1.0, 0.0
        ).astype(bf16)
        slab[0, t] = lax.dot_general(
            raw[...], move, (((1,), (1,)), ((), ())), preferred_element_type=f32).astype(bf16)
        start(s_copy(t))

    def relay(c):
        for o in range(1, G):
            z_copy(c, o).wait_recv()
            if H > 1:
                start(x_copy(c, 0, o, 1))
        step = 2
        while step < H:
            for o in range(G):
                for h in range(step):
                    if h >= step // 2:
                        x_copy(c, h - step // 2, o, step // 2).wait_recv()
                    start(x_copy(c, h, o, step))
            step *= 2

    def score(c):
        half = H // 2
        for h in range(half, H):
            if h:
                for o in range(G):
                    x_copy(c, h - half, o, half).wait_recv()
        if c == 0:
            for t in range(tiles):
                s_copy(t).wait_recv()
        part = G * R

        for h0 in range(H):
            if H > 2 or h0 == 0:
                span = part if H > 2 else H * part
                x = rows[c, pl.ds(h0 * part, span)]
                best = None
                for side in range(2):
                    for t in range(tiles):
                        sc = jnp.dot(x, slab[side, t], preferred_element_type=f32)
                        top = jnp.maximum(sc[:, :BINS], sc[:, BINS:])
                        best = top if best is None else jnp.maximum(best, top)
                for i in range(span // part):
                    h = h0 + i
                    piece = best[i * part:(i + 1) * part]
                    if h == 0:
                        own[c] = piece
                    else:
                        xout[c, h - 1] = piece
                        start(xb_copy(c, h))

    def combine(c):
        total = own[c]
        for h in range(1, H):
            xb_copy(c, h).wait_recv()
            total = jnp.maximum(total, xin[c, h - 1])
        back[c] = total
        ans[c, pl.ds(0, R)] = total[:R]
        for o in range(G - 1, 0, -1):
            start(zb_copy(c, o))

    for step in range(C + 2):
        if step < C:
            relay(step)
        if 0 <= step - 1 < C:
            score(step - 1)
        if 0 <= step - 2 < C:
            combine(step - 2)

    total = None
    for c in range(C):
        for o in range(1, G):
            zb_copy(c, o).wait_recv()
        value = ans[c]
        high = value.astype(bf16)
        low = (value - high.astype(f32)).astype(bf16)
        got = lax.dot_general(
            chooser[pl.ds(c * G * R, G * R), :], jnp.concatenate([high, low], axis=1),
            (((0,), (0,)), ((), ())), preferred_element_type=f32)
        total = got if total is None else total + got
    out_ref[...] = total[:, :BINS] + total[:, BINS:]
    for copy in started:
        copy.wait_send()


def per_device(queries, projection, vectors, bins, routes):
    G, NB = lax.axis_size("db"), lax.axis_size("blk")
    n, depth = queries.shape
    width = vectors.shape[1]
    cap = 2 * n // G
    C = 4 if cap % 64 == 0 else 1
    R = cap // C
    H = NB // 2
    tiles = width // TILE
    f32, bf16 = jnp.float32, jnp.bfloat16
    anyspace = pl.BlockSpec(memory_space=pl.ANY)
    vmem = pl.BlockSpec(memory_space=pltpu.VMEM)
    dma = pltpu.SemaphoreType.DMA
    out = pl.pallas_call(
        functools.partial(kernel, G, NB, C, R),
        out_shape=jax.ShapeDtypeStruct((n, BINS), f32),
        in_specs=[anyspace, anyspace, anyspace, vmem, vmem],
        out_specs=vmem,
        scratch_shapes=[
            pltpu.VMEM((n, depth), bf16),
            pltpu.VMEM(projection.shape, bf16),
            pltpu.VMEM((depth, width), bf16),
            pltpu.VMEM((2, tiles, depth, TILE), bf16),
            pltpu.VMEM((C * G * R, n), bf16),
            pltpu.VMEM((C, G * R, depth), bf16),
            pltpu.VMEM((C, H * G * R, depth), bf16),
            pltpu.VMEM((C, G * R, BINS), f32),
            pltpu.VMEM((C, max(1, H - 1), G * R, BINS), f32),
            pltpu.VMEM((C, max(1, H - 1), G * R, BINS), f32),
            pltpu.VMEM((C, G * R, BINS), f32),
            pltpu.VMEM((C, G * R, BINS), f32),
            dma((3,)),
            dma((C, G)), dma((C, G)),
            dma((C, H, G)), dma((C, H, G)),
            dma((tiles,)), dma((tiles,)),
            dma((C, H)), dma((C, H)),
            dma((C, G)), dma((C, G)),
        ],
        compiler_params=pltpu.CompilerParams(
            collective_id=0, has_side_effects=True, vmem_limit_bytes=48 * 1024 * 1024),
    )(queries, projection, vectors, bins.reshape(1, -1), routes.reshape(1, -1))
    return logit_scale * out


def solution(mesh):
    in_specs = (
        P(("parts", "db", "blk"), None),
        P(),
        P(None, ("parts", "db", "blk")),
        P(("parts", "db", "blk")),
        P(("parts", "db", "blk"), None),
    )
    out_specs = P(("parts", "db", "blk"), None)
    return jax.shard_map(
        per_device, mesh=mesh, in_specs=in_specs, out_specs=out_specs, check_vma=False
    )
```

```python
import functools

import jax
import jax.numpy as jnp
from jax import lax
from jax.experimental import pallas as pl
from jax.experimental.pallas import tpu as pltpu
from jax.sharding import PartitionSpec as P

BINS = 128
TILE = 256
logit_scale = 10.0
MESH = pl.DeviceIdType.MESH


CODE_SCALE = 2.0 ** 26


def encode(score):
    scaled = score * CODE_SCALE
    square = scaled * scaled
    fourth = square * square
    return jnp.where(score < 0, -fourth, fourth)


def decode(code):
    root = jnp.sqrt(jnp.sqrt(jnp.abs(code))) * (1.0 / CODE_SCALE)
    return jnp.where(code < 0, -root, root)


def kernel(
    G, NB, C, R,
    q_hbm, p_hbm, v_hbm, b_hbm, r_hbm,
    out_ref,
    q_ref, p_ref, raw, bins_ref, routes_ref, slab, chooser, outgoing, rows, own, xout, xin, back, ans,
    load_sem, z_ss, z_rs, x_ss, x_rs, s_ss, s_rs, xb_ss, xb_rs, zb_ss, zb_rs,
):
    H = NB // 2
    n, depth = q_ref.shape
    width = raw.shape[1]
    tiles = width // TILE
    f32, bf16 = jnp.float32, jnp.bfloat16
    d = lax.axis_index("db")
    k = lax.axis_index("blk")

    loads = [
        pltpu.make_async_copy(r_hbm, routes_ref, load_sem.at[0]),
        pltpu.make_async_copy(q_hbm, q_ref, load_sem.at[1]),
        pltpu.make_async_copy(p_hbm, p_ref, load_sem.at[2]),
        pltpu.make_async_copy(b_hbm, bins_ref, load_sem.at[3]),
        pltpu.make_async_copy(v_hbm, raw, load_sem.at[4]),
    ]
    for load in loads:
        load.start()

    barrier = pltpu.get_barrier_semaphore()
    for o in range(1, G):
        pl.semaphore_signal(barrier, inc=1, device_id={"db": d ^ o}, device_id_type=MESH)
    for h in range(1, H):
        pl.semaphore_signal(barrier, inc=1, device_id={"blk": k ^ (2 * h)}, device_id_type=MESH)
    pl.semaphore_signal(barrier, inc=1, device_id={"blk": k ^ 1}, device_id_type=MESH)

    def block(c, h, o):
        return rows.at[c, pl.ds((h * G + o) * R, R)]

    def z_copy(c, o):
        return pltpu.make_async_remote_copy(
            src_ref=outgoing.at[c, pl.ds(o * R, R)], dst_ref=block(c, 0, o),
            send_sem=z_ss.at[c, o], recv_sem=z_rs.at[c, o],
            device_id={"db": d ^ o}, device_id_type=MESH)

    def x_copy(c, h, o, step):
        return pltpu.make_async_remote_copy(
            src_ref=block(c, h, o), dst_ref=block(c, h + step, o),
            send_sem=x_ss.at[c, h + step, o], recv_sem=x_rs.at[c, h + step, o],
            device_id={"blk": k ^ (2 * step)}, device_id_type=MESH)

    def s_copy(t):
        return pltpu.make_async_remote_copy(
            src_ref=slab.at[0, t], dst_ref=slab.at[1, t],
            send_sem=s_ss.at[t], recv_sem=s_rs.at[t],
            device_id={"blk": k ^ 1}, device_id_type=MESH)

    def xb_copy(c, h):
        return pltpu.make_async_remote_copy(
            src_ref=xout.at[c, h - 1], dst_ref=xin.at[c, h - 1],
            send_sem=xb_ss.at[c, h], recv_sem=xb_rs.at[c, h],
            device_id={"blk": k ^ (2 * h)}, device_id_type=MESH)

    def zb_copy(c, o):
        return pltpu.make_async_remote_copy(
            src_ref=back.at[c, pl.ds(o * R, R)], dst_ref=ans.at[c, pl.ds(o * R, R)],
            send_sem=zb_ss.at[c, o], recv_sem=zb_rs.at[c, o],
            device_id={"db": d ^ o}, device_id_type=MESH)

    started = []

    def start(copy):
        copy.start()
        started.append(copy)

    loads[0].wait()
    target = routes_ref[...]
    pad = max(8, G)
    hot = jnp.where(lax.broadcasted_iota(jnp.int32, (pad, n), 0) == target, 1.0, 0.0)
    before = jnp.where(
        lax.broadcasted_iota(jnp.int32, (n, n), 0) < lax.broadcasted_iota(jnp.int32, (n, n), 1),
        1.0, 0.0).astype(bf16)
    earlier = jnp.dot(hot.astype(bf16), before, preferred_element_type=f32)
    slot = jnp.sum(hot * earlier, axis=0, keepdims=True).astype(jnp.int32)
    position = (slot // R) * (G * R) + (target ^ d) * R + slot % R

    loads[1].wait()
    loads[2].wait()
    projected = jnp.dot(q_ref[...], p_ref[...], preferred_element_type=f32)
    normed = (
        projected * lax.rsqrt(jnp.sum(projected * projected, axis=1, keepdims=True) + 1e-06)
    ).astype(bf16)

    pl.semaphore_wait(barrier, G - 1 + H)

    for c in range(C):
        pick = jnp.where(
            lax.broadcasted_iota(jnp.int32, (G * R, n), 0) + c * G * R == position, 1.0, 0.0
        ).astype(bf16)
        chooser[pl.ds(c * G * R, G * R), :] = pick
        chosen = jnp.dot(pick, normed, preferred_element_type=f32).astype(bf16)
        outgoing[c] = chosen
        rows[c, pl.ds(0, R)] = chosen[:R]
        for o in range(G - 1, 0, -1):
            start(z_copy(c, o))
        if H > 1:
            start(x_copy(c, 0, 0, 1))

    loads[3].wait()
    loads[4].wait()
    bins = bins_ref[...]
    inner = jnp.where(
        lax.broadcasted_iota(jnp.int32, (BINS, BINS), 0)
        < lax.broadcasted_iota(jnp.int32, (BINS, BINS), 1), 1.0, 0.0).astype(bf16)
    run = jnp.zeros((BINS, 1), f32)
    places = []
    for s in range(width // BINS):
        mine = bins[:, s * BINS:(s + 1) * BINS]
        hot = jnp.where(lax.broadcasted_iota(jnp.int32, (BINS, BINS), 0) == mine, 1.0, 0.0)
        earlier = jnp.dot(hot.astype(bf16), inner, preferred_element_type=f32) + run
        rank = jnp.sum(hot * earlier, axis=0, keepdims=True).astype(jnp.int32)
        places.append(rank * BINS + mine)
        run = run + jnp.sum(hot, axis=1, keepdims=True)
    place = jnp.concatenate(places, axis=1)
    for t in range(tiles):
        move = jnp.where(
            lax.broadcasted_iota(jnp.int32, (TILE, width), 0) + t * TILE == place, 1.0, 0.0
        ).astype(bf16)
        slab[0, t] = lax.dot_general(
            raw[...], move, (((1,), (1,)), ((), ())), preferred_element_type=f32).astype(bf16)
        start(s_copy(t))

    def relay(c):
        for o in range(1, G):
            z_copy(c, o).wait_recv()
            if H > 1:
                start(x_copy(c, 0, o, 1))
        step = 2
        while step < H:
            for o in range(G):
                for h in range(step):
                    if h >= step // 2:
                        x_copy(c, h - step // 2, o, step // 2).wait_recv()
                    start(x_copy(c, h, o, step))
            step *= 2

    def score(c):
        half = H // 2
        for h in range(half, H):
            if h:
                for o in range(G):
                    x_copy(c, h - half, o, half).wait_recv()
        if c == 0:
            for t in range(tiles):
                s_copy(t).wait_recv()
        part = G * R

        for h0 in range(H):
            if H > 2 or h0 == 0:
                span = part if H > 2 else H * part
                x = rows[c, pl.ds(h0 * part, span)]
                best = None
                for side in range(2):
                    for t in range(tiles):
                        sc = jnp.dot(x, slab[side, t], preferred_element_type=f32)
                        top = jnp.maximum(sc[:, :BINS], sc[:, BINS:])
                        best = top if best is None else jnp.maximum(best, top)
                best = encode(best).astype(bf16)
                for i in range(span // part):
                    h = h0 + i
                    piece = best[i * part:(i + 1) * part]
                    if h == 0:
                        own[c] = piece
                    else:
                        xout[c, h - 1] = piece
                        start(xb_copy(c, h))

    def combine(c):
        total = own[c]
        for h in range(1, H):
            xb_copy(c, h).wait_recv()
            total = jnp.maximum(total, xin[c, h - 1])
        back[c] = total
        ans[c, pl.ds(0, R)] = total[:R]
        for o in range(G - 1, 0, -1):
            start(zb_copy(c, o))

    for step in range(C + 2):
        if step < C:
            relay(step)
        if 0 <= step - 1 < C:
            score(step - 1)
        if 0 <= step - 2 < C:
            combine(step - 2)

    total = None
    for c in range(C):
        for o in range(1, G):
            zb_copy(c, o).wait_recv()
        got = lax.dot_general(
            chooser[pl.ds(c * G * R, G * R), :], ans[c], (((0,), (0,)), ((), ())),
            preferred_element_type=f32)
        total = got if total is None else total + got
    out_ref[...] = decode(total)
    for copy in started:
        copy.wait_send()


def per_device(queries, projection, vectors, bins, routes):
    G, NB = lax.axis_size("db"), lax.axis_size("blk")
    n, depth = queries.shape
    width = vectors.shape[1]
    cap = 2 * n // G
    C = 4 if cap % 64 == 0 else 1
    R = cap // C
    H = NB // 2
    tiles = width // TILE
    f32, bf16 = jnp.float32, jnp.bfloat16
    hbm = pl.BlockSpec(memory_space=pltpu.HBM)
    vmem = pl.BlockSpec(memory_space=pltpu.VMEM)
    dma = pltpu.SemaphoreType.DMA
    out = pl.pallas_call(
        functools.partial(kernel, G, NB, C, R),
        out_shape=jax.ShapeDtypeStruct((n, BINS), f32),
        in_specs=[hbm] * 5,
        out_specs=vmem,
        scratch_shapes=[
            pltpu.VMEM((n, depth), bf16),
            pltpu.VMEM(projection.shape, bf16),
            pltpu.VMEM((depth, width), bf16),
            pltpu.VMEM((1, width), jnp.int32),
            pltpu.VMEM((1, n), jnp.int32),
            pltpu.VMEM((2, tiles, depth, TILE), bf16),
            pltpu.VMEM((C * G * R, n), bf16),
            pltpu.VMEM((C, G * R, depth), bf16),
            pltpu.VMEM((C, H * G * R, depth), bf16),
            pltpu.VMEM((C, G * R, BINS), bf16),
            pltpu.VMEM((C, max(1, H - 1), G * R, BINS), bf16),
            pltpu.VMEM((C, max(1, H - 1), G * R, BINS), bf16),
            pltpu.VMEM((C, G * R, BINS), bf16),
            pltpu.VMEM((C, G * R, BINS), bf16),
            dma((5,)),
            dma((C, G)), dma((C, G)),
            dma((C, H, G)), dma((C, H, G)),
            dma((tiles,)), dma((tiles,)),
            dma((C, H)), dma((C, H)),
            dma((C, G)), dma((C, G)),
        ],
        compiler_params=pltpu.CompilerParams(
            collective_id=0, has_side_effects=True, vmem_limit_bytes=63 * 1024 * 1024),
    )(queries, projection, vectors, bins.reshape(1, -1), routes.reshape(1, -1))
    return logit_scale * out


def solution(mesh):
    in_specs = (
        P(("parts", "db", "blk"), None),
        P(),
        P(None, ("parts", "db", "blk")),
        P(("parts", "db", "blk")),
        P(("parts", "db", "blk"), None),
    )
    out_specs = P(("parts", "db", "blk"), None)
    return jax.shard_map(
        per_device, mesh=mesh, in_specs=in_specs, out_specs=out_specs, check_vma=False
    )
```

```python
import functools

import jax
import jax.numpy as jnp
from jax import lax
from jax.experimental import pallas as pl
from jax.experimental.pallas import tpu as pltpu
from jax.sharding import PartitionSpec as P

BINS = 128
TILE = 256
logit_scale = 10.0
MESH = pl.DeviceIdType.MESH


CODE_SCALE = 2.0 ** 26


def encode(score):
    scaled = score * CODE_SCALE
    square = scaled * scaled
    fourth = square * square
    return jnp.where(score < 0, -fourth, fourth)


def decode(code):
    root = jnp.sqrt(jnp.sqrt(jnp.abs(code))) * (1.0 / CODE_SCALE)
    return jnp.where(code < 0, -root, root)


def kernel(
    G, NB, sizes,
    q_hbm, p_hbm, v_hbm, b_hbm, r_hbm,
    out_ref,
    q_ref, p_ref, raw, bins_ref, routes_ref, slab, chooser, outgoing, rows, own, xout, xin, back, ans,
    load_sem, z_ss, z_rs, x_ss, x_rs, s_ss, s_rs, xb_ss, xb_rs, zb_ss, zb_rs,
):
    H = NB // 2
    C = len(sizes)
    firsts = [sum(sizes[:c]) for c in range(C)]
    n, depth = q_ref.shape
    width = raw.shape[1]
    tiles = width // TILE
    f32, bf16 = jnp.float32, jnp.bfloat16
    d = lax.axis_index("db")
    k = lax.axis_index("blk")

    loads = [
        pltpu.make_async_copy(r_hbm, routes_ref, load_sem.at[0]),
        pltpu.make_async_copy(q_hbm, q_ref, load_sem.at[1]),
        pltpu.make_async_copy(p_hbm, p_ref, load_sem.at[2]),
        pltpu.make_async_copy(b_hbm, bins_ref, load_sem.at[3]),
        pltpu.make_async_copy(v_hbm, raw, load_sem.at[4]),
    ]
    for load in loads:
        load.start()

    barrier = pltpu.get_barrier_semaphore()
    for o in range(1, G):
        pl.semaphore_signal(barrier, inc=1, device_id={"db": d ^ o}, device_id_type=MESH)
    for h in range(1, H):
        pl.semaphore_signal(barrier, inc=1, device_id={"blk": k ^ (2 * h)}, device_id_type=MESH)
    pl.semaphore_signal(barrier, inc=1, device_id={"blk": k ^ 1}, device_id_type=MESH)

    def block(c, h, o):
        return rows.at[pl.ds(H * G * firsts[c] + (h * G + o) * sizes[c], sizes[c])]

    def part(c, o):
        return pl.ds(G * firsts[c] + o * sizes[c], sizes[c])

    def whole(c):
        return pl.ds(G * firsts[c], G * sizes[c])

    def z_copy(c, o):
        return pltpu.make_async_remote_copy(
            src_ref=outgoing.at[part(c, o)], dst_ref=block(c, 0, o),
            send_sem=z_ss.at[c, o], recv_sem=z_rs.at[c, o],
            device_id={"db": d ^ o}, device_id_type=MESH)

    def x_copy(c, h, o, step):
        return pltpu.make_async_remote_copy(
            src_ref=block(c, h, o), dst_ref=block(c, h + step, o),
            send_sem=x_ss.at[c, h + step, o], recv_sem=x_rs.at[c, h + step, o],
            device_id={"blk": k ^ (2 * step)}, device_id_type=MESH)

    def s_copy(t):
        return pltpu.make_async_remote_copy(
            src_ref=slab.at[0, t], dst_ref=slab.at[1, t],
            send_sem=s_ss.at[t], recv_sem=s_rs.at[t],
            device_id={"blk": k ^ 1}, device_id_type=MESH)

    def xb_copy(c, h):
        return pltpu.make_async_remote_copy(
            src_ref=xout.at[h - 1, whole(c)], dst_ref=xin.at[h - 1, whole(c)],
            send_sem=xb_ss.at[c, h], recv_sem=xb_rs.at[c, h],
            device_id={"blk": k ^ (2 * h)}, device_id_type=MESH)

    def zb_copy(c, o):
        return pltpu.make_async_remote_copy(
            src_ref=back.at[part(c, o)], dst_ref=ans.at[part(c, o)],
            send_sem=zb_ss.at[c, o], recv_sem=zb_rs.at[c, o],
            device_id={"db": d ^ o}, device_id_type=MESH)

    started = []

    def start(copy):
        copy.start()
        started.append(copy)

    loads[0].wait()
    target = routes_ref[...]
    pad = max(8, G)
    hot = jnp.where(lax.broadcasted_iota(jnp.int32, (pad, n), 0) == target, 1.0, 0.0)
    before = jnp.where(
        lax.broadcasted_iota(jnp.int32, (n, n), 0) < lax.broadcasted_iota(jnp.int32, (n, n), 1),
        1.0, 0.0).astype(bf16)
    earlier = jnp.dot(hot.astype(bf16), before, preferred_element_type=f32)
    slot = jnp.sum(hot * earlier, axis=0, keepdims=True).astype(jnp.int32)
    position = (target ^ d) * sizes[0] + slot
    for c in range(1, C):
        position = jnp.where(
            slot < firsts[c], position,
            G * firsts[c] + (target ^ d) * sizes[c] + slot - firsts[c])

    loads[1].wait()
    loads[2].wait()
    projected = jnp.dot(q_ref[...], p_ref[...], preferred_element_type=f32)
    normed = (
        projected * lax.rsqrt(jnp.sum(projected * projected, axis=1, keepdims=True) + 1e-06)
    ).astype(bf16)

    pl.semaphore_wait(barrier, G - 1 + H)

    for c in range(C):
        pick = jnp.where(
            lax.broadcasted_iota(jnp.int32, (G * sizes[c], n), 0) + G * firsts[c] == position,
            1.0, 0.0).astype(bf16)
        chooser[whole(c), :] = pick
        chosen = jnp.dot(pick, normed, preferred_element_type=f32).astype(bf16)
        outgoing[whole(c)] = chosen
        rows[pl.ds(H * G * firsts[c], sizes[c])] = chosen[:sizes[c]]
        for o in range(1, G):
            start(z_copy(c, o))
        if H > 1:
            start(x_copy(c, 0, 0, 1))

    loads[3].wait()
    loads[4].wait()
    bins = bins_ref[...]
    inner = jnp.where(
        lax.broadcasted_iota(jnp.int32, (BINS, BINS), 0)
        < lax.broadcasted_iota(jnp.int32, (BINS, BINS), 1), 1.0, 0.0).astype(bf16)
    run = jnp.zeros((BINS, 1), f32)
    places = []
    for s in range(width // BINS):
        mine = bins[:, s * BINS:(s + 1) * BINS]
        hot = jnp.where(lax.broadcasted_iota(jnp.int32, (BINS, BINS), 0) == mine, 1.0, 0.0)
        earlier = jnp.dot(hot.astype(bf16), inner, preferred_element_type=f32) + run
        rank = jnp.sum(hot * earlier, axis=0, keepdims=True).astype(jnp.int32)
        places.append(rank * BINS + mine)
        run = run + jnp.sum(hot, axis=1, keepdims=True)
    place = jnp.concatenate(places, axis=1)
    for t in range(tiles):
        move = jnp.where(
            lax.broadcasted_iota(jnp.int32, (TILE, width), 0) + t * TILE == place, 1.0, 0.0
        ).astype(bf16)
        slab[0, t] = lax.dot_general(
            raw[...], move, (((1,), (1,)), ((), ())), preferred_element_type=f32).astype(bf16)
        start(s_copy(t))

    def relay(c):
        for o in range(1, G):
            z_copy(c, o).wait_recv()
            if H > 1:
                start(x_copy(c, 0, o, 1))
        step = 2
        while step < H:
            for o in range(G):
                for h in range(step):
                    if h >= step // 2:
                        x_copy(c, h - step // 2, o, step // 2).wait_recv()
                    start(x_copy(c, h, o, step))
            step *= 2

    def score(c):
        half = H // 2
        for h in range(half, H):
            if h:
                for o in range(G):
                    x_copy(c, h - half, o, half).wait_recv()
        if c == 0:
            for t in range(tiles):
                s_copy(t).wait_recv()
        count = G * sizes[c]
        base = H * G * firsts[c]

        for h0 in range(H):
            if H > 2 or h0 == 0:
                span = count if H > 2 else H * count
                x = rows[pl.ds(base + h0 * count, span)]
                best = None
                for side in range(2):
                    for t in range(tiles):
                        sc = jnp.dot(x, slab[side, t], preferred_element_type=f32)
                        top = jnp.maximum(sc[:, :BINS], sc[:, BINS:])
                        best = top if best is None else jnp.maximum(best, top)
                best = encode(best).astype(bf16)
                for i in range(span // count):
                    h = h0 + i
                    piece = best[i * count:(i + 1) * count]
                    if h == 0:
                        own[whole(c)] = piece
                    else:
                        xout[h - 1, whole(c)] = piece
                        start(xb_copy(c, h))

    def combine(c):
        total = own[whole(c)]
        for h in range(1, H):
            xb_copy(c, h).wait_recv()
            total = jnp.maximum(total, xin[h - 1, whole(c)])
        back[whole(c)] = total
        ans[part(c, 0)] = total[:sizes[c]]
        for o in range(G - 1, 0, -1):
            start(zb_copy(c, o))

    for step in range(C + 2):
        if step < C:
            relay(step)
        if 0 <= step - 1 < C:
            score(step - 1)
        if 0 <= step - 2 < C:
            combine(step - 2)

    total = None
    for c in range(C):
        for o in range(1, G):
            zb_copy(c, o).wait_recv()
        got = lax.dot_general(
            chooser[whole(c), :], ans[whole(c)], (((0,), (0,)), ((), ())),
            preferred_element_type=f32)
        total = got if total is None else total + got
    out_ref[...] = decode(total)
    for copy in started:
        copy.wait_send()


def per_device(queries, projection, vectors, bins, routes):
    G, NB = lax.axis_size("db"), lax.axis_size("blk")
    n, depth = queries.shape
    width = vectors.shape[1]
    cap = 2 * n // G
    unit = cap // 8
    sizes = [3 * unit, 3 * unit, 2 * unit] if cap % 128 == 0 else [cap]
    C = len(sizes)
    H = NB // 2
    tiles = width // TILE
    f32, bf16 = jnp.float32, jnp.bfloat16
    hbm = pl.BlockSpec(memory_space=pltpu.HBM)
    vmem = pl.BlockSpec(memory_space=pltpu.VMEM)
    dma = pltpu.SemaphoreType.DMA
    out = pl.pallas_call(
        functools.partial(kernel, G, NB, tuple(sizes)),
        out_shape=jax.ShapeDtypeStruct((n, BINS), f32),
        in_specs=[hbm] * 5,
        out_specs=vmem,
        scratch_shapes=[
            pltpu.VMEM((n, depth), bf16),
            pltpu.VMEM(projection.shape, bf16),
            pltpu.VMEM((depth, width), bf16),
            pltpu.VMEM((1, width), jnp.int32),
            pltpu.VMEM((1, n), jnp.int32),
            pltpu.VMEM((2, tiles, depth, TILE), bf16),
            pltpu.VMEM((G * cap, n), bf16),
            pltpu.VMEM((G * cap, depth), bf16),
            pltpu.VMEM((H * G * cap, depth), bf16),
            pltpu.VMEM((G * cap, BINS), bf16),
            pltpu.VMEM((max(1, H - 1), G * cap, BINS), bf16),
            pltpu.VMEM((max(1, H - 1), G * cap, BINS), bf16),
            pltpu.VMEM((G * cap, BINS), bf16),
            pltpu.VMEM((G * cap, BINS), bf16),
            dma((5,)),
            dma((C, G)), dma((C, G)),
            dma((C, H, G)), dma((C, H, G)),
            dma((tiles,)), dma((tiles,)),
            dma((C, H)), dma((C, H)),
            dma((C, G)), dma((C, G)),
        ],
        compiler_params=pltpu.CompilerParams(
            collective_id=0, has_side_effects=True, vmem_limit_bytes=63 * 1024 * 1024),
    )(queries, projection, vectors, bins.reshape(1, -1), routes.reshape(1, -1))
    return logit_scale * out


def solution(mesh):
    in_specs = (
        P(("parts", "db", "blk"), None),
        P(),
        P(None, ("parts", "db", "blk")),
        P(("parts", "db", "blk")),
        P(("parts", "db", "blk"), None),
    )
    out_specs = P(("parts", "db", "blk"), None)
    return jax.shard_map(
        per_device, mesh=mesh, in_specs=in_specs, out_specs=out_specs, check_vma=False
    )
```
